32 devices in a mesh: grp: 2 (over x), tm: 16 (over z, y, core).
Axes of the slice: x: 2, y: 2, z: 4, core: 2. Of those that a mesh axis runs over, the one named last changes fastest.
Arguments:
- block_input: bfloat16 [4, 16, 120, 384], P('grp', 'tm'), parts along dimension 0, may hold values from -6 to 6
- hidden_state: bfloat16 [4, 16, 120, 384], P('grp', 'tm'), parts along dimension 0, may hold values from -6 to 6
- norm_gain: float32 [384], replicated, may hold values from 0.5 to 1.5
- conv_weight: bfloat16 [3, 3, 3, 384, 384], replicated, may hold values from -0.0625 to 0.0625
- attn_gain: float32 [384], replicated, may hold values from 0.5 to 1.5
- qkv_weight: bfloat16 [384, 1152], replicated, may hold values from -4 to 4
- proj_weight: bfloat16 [384, 384], replicated, may hold values from -0.3125 to 0.3125
Outputs:
- block_output: bfloat16 [4, 16, 120, 384], P('grp', 'tm'), parts along dimension 0
The draws below stay inside these ranges and needn't reach their ends.
There are 2 independent parts, one for each index of `grp`. The reference program is written for one: setup_inputs(seed, part) draws one part's arguments, and reference() takes and returns one part's arrays. A program takes and returns all parts, laid end to end along the dimension named above; an argument that names none is the same for every part. Nothing has to cross between parts.
All inputs are finite; a program needn't handle non-finite values.
Results may differ from the reference program's by a relative error of at most 0.006.
Values may be sent and summed in bfloat16 or wider, within the bound.
A program may use at most 128 MiB of HBM per device.

```python
import jax
import jax.numpy as jnp
from jax import lax

C = 384
FRAMES = 2
COLS = 120
ROWS = 16


def draw_qkv_weight(key, part):
    first_key = jax.random.fold_in(key, 0)
    noise = jnp.clip(jax.random.normal(first_key, (C, 3 * C), jnp.float32), -4.0, 4.0) / jnp.sqrt(jnp.float32(C))
    return noise.astype(jnp.bfloat16)


def block_scale(own_key, shape, cuts, least, top_value):
    level = 1.0
    for dim, blocks in cuts:
        steps = jax.random.uniform(jax.random.fold_in(jax.random.fold_in(own_key, 6), dim), (blocks,), jnp.float32, least / len(cuts), top_value / len(cuts))
        level = level * jnp.repeat(jnp.exp(steps), shape[dim] // blocks).reshape((-1,) + (1,) * (len(shape) - 1 - dim))
    return level


def centred(rng, extent, scale, most, cuts=(), held_as=jnp.bfloat16):
    drawn = scale * jax.random.normal(rng, extent, jnp.float32)
    if cuts:
        drawn = drawn * block_scale(rng, extent, cuts, -0.22, 0.18)
    return jnp.clip(drawn, -most, most).astype(held_as)


def setup_inputs(seed: int = 0, part: int = 0) -> dict:
    arg_keys = jax.random.split(jax.random.key(seed), 8)
    part_splits = jax.random.split(jax.random.fold_in(arg_keys[7], part), 8)
    return {
        "block_input": centred(part_splits[0], (FRAMES, ROWS, COLS, C), 1.0, 6.0, ((1, 16),)),
        "hidden_state": centred(part_splits[1], (FRAMES, ROWS, COLS, C), 1.0, 6.0, ((1, 16),)),
        "norm_gain": jnp.clip(1.0 + 0.1 * jax.random.normal(arg_keys[2], (C,), jnp.float32), 0.5, 1.5),
        "conv_weight": centred(arg_keys[3], (3, 3, 3, C, C), (27 * C) ** -0.5, 0.0625),
        "attn_gain": jnp.clip(1.0 + 0.1 * jax.random.normal(arg_keys[4], (C,), jnp.float32), 0.5, 1.5),
        "qkv_weight": draw_qkv_weight(jax.random.fold_in(arg_keys[7], 71), part),
        "proj_weight": centred(arg_keys[6], (C, C), C ** -0.5, 0.3125),
    }


def rms_scale(values, gain):
    wide = values.astype(jnp.float32)
    return wide * lax.rsqrt(lax.optimization_barrier(jnp.mean(wide * wide, axis=-1, keepdims=True)) + 1e-06) * gain.astype(jnp.float32)

def conv_frame(padded, start, kernel):
    channels = padded.shape[-1]
    row_count = padded.shape[1] - 2
    col_count = padded.shape[2] - 2
    window = lax.dynamic_slice_in_dim(padded, start.astype(jnp.int32), 3, 0)
    pieces = [window[t_off, r_off:r_off + row_count, c_off:c_off + col_count, :] for t_off in range(3) for r_off in range(3) for c_off in range(3)]
    stacked = jnp.concatenate(pieces, axis=-1).reshape(-1, 27 * channels)
    result = jnp.dot(stacked, kernel.reshape(27 * channels, channels), preferred_element_type=jnp.float32)
    return result.reshape(row_count, col_count, channels)

def attend(normed_frame, mixed_frame, qkv_weight, proj_weight):
    channels = normed_frame.shape[-1]
    tokens = normed_frame.reshape(-1, channels)
    projected = jnp.dot(tokens, qkv_weight, preferred_element_type=jnp.float32).astype(jnp.bfloat16)
    queries = projected[:, :channels]
    key_part = projected[:, channels:2 * channels]
    value_part = projected[:, 2 * channels:]
    scores = jnp.dot(queries, key_part.T, preferred_element_type=jnp.float32) * channels ** (-0.5)
    scores = scores - lax.optimization_barrier(jnp.max(scores, axis=-1, keepdims=True))
    expo = jnp.exp(scores)
    weights = (expo / lax.optimization_barrier(jnp.sum(expo, axis=-1, keepdims=True))).astype(jnp.bfloat16)
    attended = jnp.dot(weights, value_part, preferred_element_type=jnp.float32).astype(jnp.bfloat16)
    result = mixed_frame.reshape(-1, channels).astype(jnp.float32) + jnp.dot(attended, proj_weight, preferred_element_type=jnp.float32)
    return result.astype(jnp.bfloat16).reshape(mixed_frame.shape)

def reference(block_input, hidden_state, norm_gain, conv_weight, attn_gain, qkv_weight, proj_weight):
    conv_in = jax.nn.silu(rms_scale(hidden_state, norm_gain)).astype(jnp.bfloat16)
    padded = jnp.pad(conv_in, ((2, 0), (1, 1), (1, 1), (0, 0)))
    frame_ids = jnp.arange(block_input.shape[0], dtype=jnp.int32)
    conv_out = lax.map(lambda start: conv_frame(padded, start, conv_weight), frame_ids)
    mixed = (block_input.astype(jnp.float32) + conv_out).astype(jnp.bfloat16)
    normed = rms_scale(mixed, attn_gain).astype(jnp.bfloat16)
    return lax.map(lambda pair: attend(pair[0], pair[1], qkv_weight, proj_weight), (normed, mixed))
```

```python
import functools

import jax
import jax.numpy as jnp
from jax import lax
from jax.experimental import pallas as pl
from jax.experimental.pallas import tpu as pltpu
from jax.sharding import PartitionSpec as P

MESH = pl.DeviceIdType.MESH
BF16 = jnp.bfloat16
F32 = jnp.float32
SLOT = 128
EPS = 1e-06


def mm(a, b):
    return jnp.dot(a, b, preferred_element_type=F32)


def mm_t(a, b):
    return lax.dot_general(a, b, (((1,), (1,)), ((), ())), preferred_element_type=F32)


def rms(wide, gain):
    return wide * lax.rsqrt(jnp.mean(wide * wide, axis=-1, keepdims=True) + EPS) * gain


def kernel(
    n, depth, hid, bi, ng, ag, cw, qkvw, projw, out,
    hal, biv, wv, qkv, proj, x2, acc, mixed, xbuf, gath, oacc, abuf, arecv,
    in_sem, w_sem, halo_send, halo_recv, pair_send, pair_recv, ring_send, ring_recv,
):
    cols, channels = hid.shape[2], hid.shape[3]
    chips = n // 2
    half = chips // 2
    me = lax.axis_index("tm")
    core, chip = me % 2, me // 2
    partner = me + 1 - 2 * core

    def to_pos(c):
        if depth == 1:
            return c
        z, y = c // 2, c % 2
        return z + y * (chips - 1 - 2 * z)

    def to_dev(p):
        if depth == 1:
            return 2 * p + core
        y = p // (chips // 2)
        z = p + y * (chips - 1 - 2 * p)
        return 2 * (2 * z + y) + core

    pos = to_pos(chip)
    right, left = to_dev((pos + 1) % chips), to_dev((pos + chips - 1) % chips)

    loads = [
        pltpu.make_async_copy(hid.at[:, 0], hal.at[1], in_sem.at[0]),
        pltpu.make_async_copy(bi.at[:, 0], biv, in_sem.at[1]),
        pltpu.make_async_copy(qkvw, qkv, in_sem.at[2]),
        pltpu.make_async_copy(projw, proj, in_sem.at[3]),
    ]
    loads[0].start()
    taps = {}
    for b in (1, 0, 2):
        for a in range(2):
            for e in range(3):
                taps[b, a, e] = pltpu.make_async_copy(
                    cw.at[2 - a, b, e],
                    wv.at[b, pl.ds(a * channels, channels), pl.ds(e * channels, channels)],
                    w_sem.at[b, a, e],
                )
    for e in range(3):
        taps[1, 0, e].start()
        taps[1, 1, e].start()
    for copy in loads[1:]:
        copy.start()

    tail = SLOT - 16
    gath[:, :, tail:, :] = jnp.zeros((chips, 2, 16, channels), BF16)

    @pl.when(me == 0)
    def _():
        hal[0] = jnp.zeros(hal.shape[1:], BF16)

    @pl.when(me == n - 1)
    def _():
        hal[2] = jnp.zeros(hal.shape[1:], BF16)

    barrier = pltpu.get_barrier_semaphore()

    def greet(d):
        pl.semaphore_signal(barrier, inc=1, device_id={"tm": d}, device_id_type=MESH)

    across = me - 1 + 2 * core
    inside = jnp.logical_and(across >= 0, across < n)
    greet(partner)
    greet(right)
    greet(left)

    @pl.when(inside)
    def _():
        greet(across)

    has_across = core * ((2 * n - 2 - me) // n) + (1 - core) * ((me + n - 1) // n)
    pl.semaphore_wait(barrier, 3 + has_across)

    def remote(src, dst, send, recv, d):
        return pltpu.make_async_remote_copy(
            src_ref=src, dst_ref=dst, send_sem=send, recv_sem=recv,
            device_id={"tm": d}, device_id_type=MESH,
        )

    down = remote(hid.at[:, 0], hal.at[0], halo_send.at[0], halo_recv.at[0], me + 1)
    up = remote(hid.at[:, 0], hal.at[2], halo_send.at[1], halo_recv.at[1], me - 1)

    @pl.when(me < n - 1)
    def _():
        down.start()

    @pl.when(me > 0)
    def _():
        up.start()

    for b in (0, 2):
        for e in range(3):
            taps[b, 0, e].start()
            taps[b, 1, e].start()

    gain = ng[...]

    def tap_row(b, first):
        wide = hal[b].astype(F32).reshape(2 * cols, channels)
        scaled = rms(wide, gain)
        act = scaled / (1.0 + jnp.exp(-scaled))
        x2[:, :channels] = act.astype(BF16)
        earlier = jnp.concatenate([jnp.zeros((cols, channels), F32), act[:cols]], axis=0)
        x2[:, channels:] = earlier.astype(BF16)
        for a in range(2):
            for e in range(3):
                taps[b, a, e].wait()
        part = mm(x2[...], wv[b])
        if first:
            acc[...] = part
        else:
            acc[...] += part

    loads[0].wait()
    tap_row(1, True)

    @pl.when(me > 0)
    def _():
        down.wait_recv()

    tap_row(0, False)

    @pl.when(me < n - 1)
    def _():
        up.wait_recv()

    tap_row(2, False)

    place = lax.broadcasted_iota(jnp.int32, (2 * cols, channels), 0)
    place = jnp.where(place >= cols, place - cols, place)
    before = pltpu.roll(acc[:, :channels], 1, 0)
    after = pltpu.roll(acc[:, 2 * channels :], 2 * cols - 1, 0)
    conv = acc[:, channels : 2 * channels]
    conv = conv + jnp.where(place == 0, 0.0, before)
    conv = conv + jnp.where(place == cols - 1, 0.0, after)
    loads[1].wait()
    total = biv[...].astype(F32).reshape(2 * cols, channels) + conv
    total = total.astype(BF16).astype(F32)
    mixed[...] = total.reshape(2, cols, channels)
    normed = rms(total, ag[...])
    is_first = core == 0
    mine = jnp.where(is_first, normed[:cols], normed[cols:]).astype(BF16)
    other = jnp.where(is_first, normed[cols:], normed[:cols]).astype(BF16)
    span = pl.ds(0, cols)
    xbuf[...] = other
    swap = remote(
        xbuf, gath.at[pos, core, span], pair_send.at[0], pair_recv.at[0], partner
    )
    swap.start()
    gath[pos, core, :cols, :] = mine

    rows = (core, 1 - core)

    def ring(way, s, j):
        owner = (pos - (s - 1) + chips) % chips if way == 0 else (pos + s - 1) % chips
        slot = gath.at[owner, rows[j], span]
        return remote(
            slot, slot, ring_send.at[way, s - 1, j], ring_recv.at[way, s - 1, j],
            right if way == 0 else left,
        )

    def carried(way, s, j):
        return s < half or (s == half and j == way)

    started = []

    def push(way, s, j):
        if s <= half and carried(way, s, j):
            copy = ring(way, s, j)
            copy.start()
            started.append(copy)

    push(0, 1, 0)
    push(1, 1, 0)
    swap.wait_recv()
    push(0, 1, 1)
    push(1, 1, 1)

    loads[2].wait()
    tokens = gath[pos].reshape(2 * SLOT, channels)
    queries = mm(tokens, qkv[:, :channels]).astype(BF16)
    folded = mm_t(queries, qkv[:, channels : 2 * channels]).astype(BF16)
    key_at = lax.broadcasted_iota(jnp.int32, (1, 2 * SLOT), 1) % SLOT
    bias = jnp.where(key_at < cols, 0.0, -1e30).astype(F32)
    scale = channels ** (-0.5)

    def unit(owner, state):
        block = gath[owner].reshape(2 * SLOT, channels)
        scores = mm_t(folded, block) * scale + bias
        top = jnp.max(scores, axis=-1, keepdims=True)
        if state is None:
            expo = jnp.exp(scores - top)
            oacc[...] = mm(expo.astype(BF16), block)
            return top, jnp.sum(expo, axis=-1, keepdims=True)
        old, mass = state
        top = jnp.maximum(old, top)
        fade = jnp.exp(old - top)
        expo = jnp.exp(scores - top)
        oacc[...] = oacc[...] * fade + mm(expo.astype(BF16), block)
        return top, mass * fade + jnp.sum(expo, axis=-1, keepdims=True)

    state = unit(pos, None)
    for s in range(1, half + 1):
        for j in range(2):
            for way in range(2):
                if carried(way, s, j):
                    ring(way, s, j).wait_recv()
                    push(way, s + 1, j)
        state = unit((pos - s + chips) % chips, state)
        if s < half:
            state = unit((pos + s) % chips, state)

    pooled = (oacc[...] / state[1]).astype(BF16)
    attended = mm(pooled, qkv[:, 2 * channels :])
    low, high = attended[:cols], attended[SLOT : SLOT + cols]
    abuf[...] = jnp.where(is_first, high, low).astype(BF16)
    back = remote(abuf, arecv, pair_send.at[1], pair_recv.at[1], partner)
    back.start()
    loads[3].wait()
    own = jnp.where(is_first, low, high).astype(BF16)
    out[core, 0] = (mixed[core] + mm(own, proj[...])).astype(BF16)
    back.wait_recv()
    out[1 - core, 0] = (mixed[1 - core] + mm(arecv[...], proj[...])).astype(BF16)

    @pl.when(me < n - 1)
    def _():
        down.wait_send()

    @pl.when(me > 0)
    def _():
        up.wait_send()

    swap.wait_send()
    back.wait_send()
    for copy in started:
        copy.wait_send()


def body(n, depth, block_input, hidden_state, norm_gain, conv_weight, attn_gain, qkv_weight, proj_weight):
    frames, _, cols, channels = block_input.shape
    chips = n // 2
    any_spec = pl.BlockSpec(memory_space=pl.ANY)
    vmem_spec = pl.BlockSpec(memory_space=pltpu.VMEM)
    dma = pltpu.SemaphoreType.DMA
    return pl.pallas_call(
        functools.partial(kernel, n, depth),
        out_shape=jax.ShapeDtypeStruct(block_input.shape, BF16),
        in_specs=[any_spec, any_spec, vmem_spec, vmem_spec, any_spec, any_spec, any_spec],
        out_specs=vmem_spec,
        scratch_shapes=[
            pltpu.VMEM((3, frames, cols, channels), BF16),
            pltpu.VMEM((frames, cols, channels), BF16),
            pltpu.VMEM((3, 2 * channels, 3 * channels), BF16),
            pltpu.VMEM((channels, 3 * channels), BF16),
            pltpu.VMEM((channels, channels), BF16),
            pltpu.VMEM((frames * cols, 2 * channels), BF16),
            pltpu.VMEM((frames * cols, 3 * channels), F32),
            pltpu.VMEM((frames, cols, channels), F32),
            pltpu.VMEM((cols, channels), BF16),
            pltpu.VMEM((chips, 2, SLOT, channels), BF16),
            pltpu.VMEM((2 * SLOT, channels), F32),
            pltpu.VMEM((cols, channels), BF16),
            pltpu.VMEM((cols, channels), BF16),
            dma((4,)),
            dma((3, 2, 3)),
            dma((2,)),
            dma((2,)),
            dma((2,)),
            dma((2,)),
            dma((2, chips // 2, 2)),
            dma((2, chips // 2, 2)),
        ],
        compiler_params=pltpu.CompilerParams(
            collective_id=0, has_side_effects=True, vmem_limit_bytes=56 * 1024 * 1024
        ),
    )(
        hidden_state, block_input, norm_gain.reshape(1, -1), attn_gain.reshape(1, -1),
        conv_weight, qkv_weight, proj_weight,
    )


def solution(mesh):
    n = mesh.shape["tm"]
    depth = 2 if mesh.shape["grp"] == 2 else 1
    return jax.shard_map(
        functools.partial(body, n, depth),
        mesh=mesh,
        in_specs=(P("grp", "tm", None, None), P("grp", "tm", None, None), P(), P(), P(), P(), P()),
        out_specs=P("grp", "tm", None, None),
        check_vma=False,
    )
```
